32 devices in a mesh: strip: 2 (over x), row: 16 (over z, y, core).
Axes of the slice: x: 2, y: 2, z: 4, core: 2. Of those that a mesh axis runs over, the one named last changes fastest.
Arguments:
- mask: float32 [512, 256], P(('strip', 'row')), parts along dimension 0, may hold values from 0 to 1
- target: float32 [512, 256], P(('strip', 'row')), parts along dimension 0, may hold values from 0 to 1
- kernels: bfloat16 [9, 24, 17, 17], replicated, may hold values from -0.375 to 0.375
- corner_weights: float32 [9, 12], replicated, may hold values from 0.03 to 0.3
- hotspots: int32 [32, 5], P('strip'), parts along dimension 0, may hold values from 0 to 8, as said below
- counts: int32 [32], P('strip'), parts along dimension 0, may hold values from 1 to 5, as said below
Outputs:
- updated_mask: float32 [512, 256], P(('strip', 'row')), parts along dimension 0
The draws below stay inside these ranges and needn't reach their ends.
There are 2 independent parts, one for each index of `strip`. The reference program is written for one: setup_inputs(seed, part) draws one part's arguments, and reference() takes and returns one part's arrays. A program takes and returns all parts, laid end to end along the dimension named above; an argument that names none is the same for every part. Nothing has to cross between parts.
Inputs may be any that keep to these rules, and one draw needn't show every extreme that they name: `hotspots`: each row names 5 distinct corners. `counts`: some tile has 5 in every draw; tiles t and t xor (8) together use at most 6 corners, and some such pair reaches it in every draw.
All inputs are finite; a program needn't handle non-finite values.
Results may differ from the reference program's by a relative error of at most 0.0062.
Values may be sent and summed in bfloat16 or wider, within the bound.
A program may use at most 64 MiB of HBM per device.

```python
import math
import jax
import jax.numpy as jnp
from jax import lax

K = 12
KS = 17
CORNERS = 9
SLOTS = 5
ITERS = 2
TR = 16
W = 256
NX = 256
N_ROW = 16


def draw_hotspots(key, part):
    keys = jax.random.split(jax.random.fold_in(key, 11), N_ROW)
    rows = jax.vmap(lambda row_key: jax.random.permutation(row_key, CORNERS)[:SLOTS])(keys)
    return rows.astype(jnp.int32)


def draw_counts(key, part):
    base = jax.random.fold_in(key, 23)
    half = N_ROW // 2
    heavy = jax.random.randint(jax.random.fold_in(base, 1), (half,), 0, 2) == 0
    place = jax.random.randint(jax.random.fold_in(base, 3), (), 0, half)
    heavy = heavy.at[place].set(True)
    side = jax.random.randint(jax.random.fold_in(base, 4), (half,), 0, 2)
    low_light = jax.random.randint(jax.random.fold_in(base, 2), (half,), 1, 4)
    high_light = jax.random.randint(jax.random.fold_in(base, 5), (half,), 1, 4)
    low = jnp.where(heavy, jnp.where(side == 0, SLOTS, 1), low_light)
    high = jnp.where(heavy, jnp.where(side == 0, 1, SLOTS), high_light)
    return jnp.concatenate([low, high]).astype(jnp.int32)


def shard_levels(key, shape, cuts, low, largest):
    gain, own = 1.0, jax.random.fold_in(key, 6)
    for position, shards_of in cuts:
        draws = jnp.exp(jax.random.uniform(jax.random.fold_in(own, position), (shards_of,), jnp.float32, low / len(cuts), largest / len(cuts)))
        gain = gain * jnp.repeat(draws, shape[position] // shards_of).reshape([-1 if axis == position else 1 for axis in range(len(shape))])
    return gain


def noise(key, extent, deviation, most, held_as=jnp.bfloat16):
    drawn = jax.random.normal(key, extent, jnp.float32) * deviation
    return jnp.minimum(jnp.maximum(drawn, -most), most).astype(held_as)


def setup_inputs(seed: int = 0, part: int = 0) -> dict:
    arg_keys = jax.random.split(jax.random.key(seed), 7)
    own_keys = jax.random.split(jax.random.fold_in(arg_keys[6], part), 7)
    return {
        "mask": jnp.clip(1.0 * jax.random.uniform(own_keys[0], (NX, W), jnp.float32) ** shard_levels(own_keys[0], (NX, W), ((0, 16),), -0.2, 0.2), 0.0, 1.0),
        "target": jnp.clip(1.0 * jax.random.uniform(own_keys[1], (NX, W), jnp.float32) ** shard_levels(own_keys[1], (NX, W), ((0, 16),), -0.2, 0.2), 0.0, 1.0),
        "kernels": noise(arg_keys[2], (CORNERS, 2 * K, KS, KS), (KS * KS) ** -0.5, 0.375),
        "corner_weights": jnp.clip(jnp.exp(jax.random.uniform(arg_keys[3], (CORNERS, K), jnp.float32, math.log(0.03), math.log(0.3))), 0.03, 0.3),
        "hotspots": draw_hotspots(jax.random.fold_in(jax.random.fold_in(arg_keys[6], part), 71), part),
        "counts": draw_counts(jax.random.fold_in(jax.random.fold_in(arg_keys[6], part), 71), part),
    }


steepness = 4.0
threshold = 0.8
step_rate = 1.0


def corner_term(extended, target_tile, kernel_set, weights):
    radius = kernel_set.shape[-1] // 2
    width = target_tile.shape[1]
    padded = jnp.pad(extended, ((0, 0), (radius, radius))).astype(jnp.bfloat16)
    field = lax.conv_general_dilated(padded[None, None], kernel_set[:, None], (1, 1), "VALID", dimension_numbers=("NCHW", "OIHW", "NCHW"), preferred_element_type=jnp.float32)[0]
    weight_both = jnp.concatenate([weights, weights])[:, None, None]
    intensity = jnp.sum(weight_both * field * field, axis=0)
    resist = jax.nn.sigmoid(steepness * (intensity - threshold))
    slope = 2.0 * (resist - target_tile) * steepness * resist * (1.0 - resist)
    source = (2.0 * weight_both * slope[None] * field).astype(jnp.bfloat16)
    flipped = kernel_set[None, :, ::-1, ::-1]
    span = 2 * radius
    back = lax.conv_general_dilated(source[None], flipped, (1, 1), ((span, span), (span, span)), dimension_numbers=("NCHW", "OIHW", "NCHW"), preferred_element_type=jnp.float32)[0, 0]
    return back[:, radius:radius + width]


def reference(mask, target, kernels, corner_weights, hotspots, counts):
    radius = KS // 2
    field = mask
    for step in range(ITERS):
        padded = jnp.pad(field, ((radius, radius), (0, 0)))

        def tile_fn(tile, grad_pad):
            tile = jnp.asarray(tile).astype(jnp.int32)
            start = (tile * TR).astype(jnp.int32)
            extended = lax.dynamic_slice_in_dim(padded, start, TR + 2 * radius, 0)
            target_tile = lax.dynamic_slice_in_dim(target, start, TR, 0)

            def corner_fn(slot, total):
                corner = hotspots[tile, slot]
                return total + corner_term(extended, target_tile, kernels[corner], corner_weights[corner])

            zeros = jnp.zeros((TR + 2 * radius, W), jnp.float32)
            total = lax.fori_loop(jnp.int32(0), counts[tile].astype(jnp.int32), corner_fn, zeros)
            previous = lax.dynamic_slice_in_dim(grad_pad, start, TR + 2 * radius, 0)
            return lax.dynamic_update_slice_in_dim(grad_pad, previous + total, start, 0)

        grad_pad = lax.fori_loop(0, N_ROW, tile_fn, jnp.zeros((NX + 2 * radius, W), jnp.float32))
        field = field - step_rate * grad_pad[radius:radius + NX]
    return field
```

```python
import functools

import jax
import jax.numpy as jnp
from jax import lax
from jax.experimental import pallas as pl
from jax.experimental.pallas import tpu as pltpu
from jax.sharding import PartitionSpec as P

STEEPNESS = 4.0
THRESHOLD = 0.8
STEP_RATE = 1.0
LANES = 128
MESH = pl.DeviceIdType.MESH
F32, BF16 = jnp.float32, jnp.bfloat16


def cdiv(a, b):
    return -(-a // b)


def round_up(a, b):
    return cdiv(a, b) * b


class Plan:
    def __init__(self, rows, width, corners, channels, side, slots):
        self.rows, self.width, self.corners, self.channels = rows, width, corners, channels
        self.side, self.slots = side, slots
        self.radius = side // 2
        self.ext = rows + 2 * self.radius
        self.tail = 4 * self.radius
        self.deep = 3 * LANES + self.tail
        self.depth = 4 * LANES
        self.lane_step = 32
        self.packed = cdiv(side * self.lane_step, LANES) * LANES
        self.slot_rows = channels * self.radius
        self.used = slots * self.slot_rows
        self.mix = round_up(self.used, 256)


def shifted(value, by):
    width = value.shape[1]
    if by == 0:
        return value
    moved = pltpu.roll(value, by % width, 1)
    column = lax.broadcasted_iota(jnp.int32, value.shape, 1)
    keep = column >= by if by > 0 else column < width + by
    return jnp.where(keep, moved, 0.0)


def kernel(p, devices, hot_hbm, count_hbm, weight_hbm, mask_hbm, target_hbm, taps_hbm, out_ref,
           hot_ref, count_ref, weight_ref, target_ref, taps, pack, big, own_t, up_t, down_t,
           blocks, tails, source, up_source, down_source, field, total, got, far,
           load_sem, send_sem, recv_sem):
    me = lax.axis_index("row")
    r = p.radius
    has_up, has_down = me > 0, me < devices - 1
    has_up2, has_down2 = me > 1, me < devices - 2
    kinds = weight_hbm.shape[1]

    barrier = pltpu.get_barrier_semaphore()

    @pl.when(has_up)
    def _():
        pl.semaphore_signal(barrier, inc=1, device_id={"row": me - 1}, device_id_type=MESH)

    @pl.when(has_down)
    def _():
        pl.semaphore_signal(barrier, inc=1, device_id={"row": me + 1}, device_id_type=MESH)

    pairs = ((mask_hbm, field.at[pl.ds(r, p.rows)]), (target_hbm, target_ref.at[pl.ds(r, p.rows)]),
             (taps_hbm, taps), (hot_hbm, hot_ref), (count_hbm, count_ref), (weight_hbm, weight_ref))
    loads = [pltpu.make_async_copy(a, b, load_sem.at[k]) for k, (a, b) in enumerate(pairs)]
    for load in loads:
        load.start()

    def copies(stage, reach, up_src, down_src, above, below):
        up = pltpu.make_async_remote_copy(
            src_ref=up_src, dst_ref=below, send_sem=send_sem.at[stage, 0],
            recv_sem=recv_sem.at[stage, 0], device_id={"row": me - reach}, device_id_type=MESH)
        down = pltpu.make_async_remote_copy(
            src_ref=down_src, dst_ref=above, send_sem=send_sem.at[stage, 1],
            recv_sem=recv_sem.at[stage, 1], device_id={"row": me + reach}, device_id_type=MESH)
        return reach, up, down

    def start(pair):
        reach, up, down = pair

        @pl.when(me >= reach)
        def _():
            up.start()

        @pl.when(me < devices - reach)
        def _():
            down.start()

    def finish(pair):
        reach, up, down = pair

        @pl.when(me >= reach)
        def _():
            up.wait_send()
            down.wait_recv()

        @pl.when(me < devices - reach)
        def _():
            down.wait_send()
            up.wait_recv()

    def clear(ref, where):
        ref[where] = jnp.zeros(ref.at[where].shape, ref.dtype)

    @pl.when(jnp.logical_not(has_up))
    def _():
        clear(field, pl.ds(0, r))
        clear(target_ref, pl.ds(0, r))
        clear(got, 0)

    @pl.when(jnp.logical_not(has_down))
    def _():
        clear(field, pl.ds(r + p.rows, r))
        clear(target_ref, pl.ds(r + p.rows, r))
        clear(got, 1)

    @pl.when(jnp.logical_not(has_up2))
    def _():
        clear(far, 0)

    @pl.when(jnp.logical_not(has_down2))
    def _():
        clear(far, 1)

    spot = lax.broadcasted_iota(jnp.int32, (1, p.depth), 1)
    in_tail = spot >= 3 * LANES
    inside = spot & (LANES - 1)
    tap_row = jnp.where(in_tail, inside, (spot // LANES) * r + (inside & (r - 1)))
    tap_col = jnp.where(in_tail, p.side - 1, inside // r)
    wanted = jnp.where(tap_row < p.side, tap_row * p.lane_step + tap_col, -1)
    place = (lax.broadcasted_iota(jnp.int32, (p.packed, p.depth), 0) == wanted).astype(F32).astype(BF16)

    pack[...] = jnp.zeros(pack.shape, F32)
    inner = has_up & has_down

    loads[0].wait()
    loads[1].wait()

    @pl.when(inner)
    def _():
        pl.semaphore_wait(barrier, 2)

    @pl.when(jnp.logical_not(inner))
    def _():
        pl.semaphore_wait(barrier, 1)

    first = copies(0, 1, field.at[pl.ds(r, r)], field.at[pl.ds(p.rows, r)],
                   field.at[pl.ds(0, r)], field.at[pl.ds(r + p.rows, r)])
    start(first)
    aims = copies(1, 1, target_ref.at[pl.ds(r, r)], target_ref.at[pl.ds(p.rows, r)],
                  target_ref.at[pl.ds(0, r)], target_ref.at[pl.ds(r + p.rows, r)])
    start(aims)

    for load in loads[2:]:
        load.wait()

    for c in range(p.corners):
        for a in range(p.side):
            pack[pl.ds(c * p.channels, p.channels), pl.ds(a * p.lane_step, p.side)] = (
                taps[c, a].astype(F32))
    base = jnp.dot(pack[...].astype(BF16), place, preferred_element_type=F32)
    lane = lax.broadcasted_iota(jnp.int32, (1, r, LANES), 2)
    phase = lax.broadcasted_iota(jnp.int32, (1, r, LANES), 1)
    straight = (lane & (r - 1)) + phase < r
    thirds = [base[:, q * LANES : (q + 1) * LANES] for q in range(4)]
    carried = [pltpu.roll(thirds[q], LANES - r, 1) for q in range(2)]
    for c in range(p.corners):
        span = slice(c * p.channels, (c + 1) * p.channels)

        def wide(part):
            return jnp.broadcast_to(part[span][:, None, :], (p.channels, r, LANES))

        for q in range(4):
            here = wide(thirds[q])
            if q < 3:
                here = jnp.where(straight, here, wide(carried[q - 1]) if q else 0.0)
            turned = pltpu.roll(here, 0, 2, stride=1, stride_axis=1)
            big[c, :, pl.ds(q * LANES, LANES)] = turned.reshape(p.slot_rows, LANES).astype(BF16)

    up_tile, down_tile = jnp.maximum(me - 1, 0), jnp.minimum(me + 1, devices - 1)
    corners = [hot_ref[s, me] for s in range(p.slots)]
    up_corners = [hot_ref[s, up_tile] for s in range(p.slots)]
    down_corners = [hot_ref[s, down_tile] for s in range(p.slots)]
    count = count_ref[me]
    up_count = jnp.where(has_up, count_ref[up_tile], 0)
    down_count = jnp.where(has_down, count_ref[down_tile], 0)

    def turn(chosen, quarters, into):
        for q in range(p.mix // 256):
            pieces, at = [], q * 256
            while at < min((q + 1) * 256, p.used):
                s, off = at // p.slot_rows, at % p.slot_rows
                size = min(p.slot_rows - off, (q + 1) * 256 - at)
                pieces.append((chosen[s], off, size))
                at += size
            for n, quarter in enumerate(quarters):
                parts = [big[c, pl.ds(off, size), pl.ds(quarter * LANES, LANES)].astype(F32)
                         for c, off, size in pieces]
                spare = 256 - sum(size for _, _, size in pieces)
                if spare:
                    parts.append(jnp.zeros((spare, LANES), F32))
                turned = jnp.concatenate(parts, axis=0).T
                tall = p.tail if quarter == 3 else LANES
                into[pl.ds(n * LANES, tall), pl.ds(q * 256, 256)] = turned[:tall].astype(BF16)

    for ref in (source, up_source, down_source):
        if p.mix > p.used:
            clear(ref, pl.ds(p.used, p.mix - p.used))
    turn(corners, (0, 1, 2, 3), own_t)

    def fill(value, first_block, first_tail, tail_count):
        count = value.shape[0] // r
        moved = [shifted(value, r - b) for b in range(p.side)]
        for i in range(count):
            rows = slice(i * r, (i + 1) * r)
            for b in range(0, p.side - 1, 2):
                two = jnp.concatenate([moved[b][rows], moved[b + 1][rows]], axis=0)
                blocks[pl.ds((first_block + i) * LANES + b * r, 2 * r), :] = two.astype(BF16)
        last = moved[p.side - 1]
        for g in range(tail_count):
            padded = jnp.concatenate([last[g * r : (g + 3) * r], jnp.zeros((r, p.width), F32)], axis=0)
            tails[first_tail + g] = padded.astype(BF16)

    def patch(g):
        return jnp.concatenate([blocks[pl.ds(g * LANES, 3 * LANES), :], tails[g]], axis=0)

    def forward(groups, chosen, limit, aim, into):
        n = len(groups) * p.width
        patches = jnp.concatenate([patch(g) for g in groups], axis=1)
        for s in range(p.slots):
            image = jnp.dot(big[chosen[s], :, pl.ds(0, p.deep)], patches, preferred_element_type=F32)
            image = image.reshape(p.channels, r, n)
            weights = [weight_ref[chosen[s], k] for k in range(kinds)]
            intensity = jnp.zeros((r, n), F32)
            for j in range(p.channels):
                intensity = intensity + weights[j % kinds] * (image[j] * image[j])
            resist = jax.nn.sigmoid(STEEPNESS * (intensity - THRESHOLD))
            slope = 2.0 * (resist - aim) * STEEPNESS * resist * (1.0 - resist)
            slope = jnp.where(s < limit, slope, 0.0)
            scaled = [(2.0 * weights[k]) * slope for k in range(kinds)]
            sent = jnp.stack([scaled[j % kinds] * image[j] for j in range(p.channels)])
            into[pl.ds(s * p.slot_rows, p.slot_rows), :] = sent.reshape(p.slot_rows, n).astype(BF16)

    def gathered(rows_of):
        sums = 0.0
        for b in range(p.side):
            sums = sums + shifted(jnp.concatenate(rows_of(b), axis=0), b - r)
        return sums

    def third(value, w, b, base=0):
        at = (w - base) * LANES + b * r if b < p.side - 1 else (3 - base) * LANES + w * r
        return value[at : at + r]

    finish(first)
    aim = jnp.concatenate([target_ref[pl.ds((g + 1) * r, r), :] for g in range(2)], axis=1)
    fill(field[...].astype(BF16).astype(F32), 1, 1, 2)
    forward((1, 2), corners, count, aim, source)
    spread = [jnp.dot(own_t[...], source[:, pl.ds(g * p.width, p.width)], preferred_element_type=F32)
              for g in range(2)]
    lo, hi = spread
    gradient = STEP_RATE * gathered(lambda b: [
        third(lo, 0, b), third(lo, 1, b) + third(hi, 0, b), third(lo, 2, b) + third(hi, 1, b),
        third(hi, 2, b)])
    total[pl.ds(0, r), :] = gradient[:r]
    total[pl.ds(r, p.rows), :] = field[pl.ds(r, p.rows), :] - gradient[r : r + p.rows]
    total[pl.ds(r + p.rows, r), :] = gradient[r + p.rows :]
    near = copies(2, 1, total.at[pl.ds(0, 3 * r)], total.at[pl.ds(r, 3 * r)], got.at[0], got.at[1])
    start(near)
    beyond = copies(3, 2, total.at[pl.ds(0, r)], total.at[pl.ds(3 * r, r)], far.at[0], far.at[1])
    start(beyond)

    turn(up_corners, (2, 3), up_t)
    turn(down_corners, (0, 3), down_t)
    finish(aims)
    finish(near)
    above, below = got[0], got[1]
    upper = jnp.where(has_up, total[pl.ds(0, r), :], 0.0)
    lower = jnp.where(has_down, total[pl.ds(3 * r, r), :], 0.0)
    own = total[pl.ds(r, p.rows), :] - jnp.concatenate([above[2 * r :], below[:r]], axis=0)
    after = jnp.concatenate([above[r : 2 * r] - upper, own, below[r : 2 * r] - lower], axis=0)
    low = after.astype(BF16).astype(F32)
    fill(low, 1, 1, 2)
    forward((1, 2), corners, count, aim, source)
    finish(beyond)
    outer = jnp.concatenate([above[:r] - far[0], low[: 2 * r]], axis=0).astype(BF16).astype(F32)
    fill_low = outer
    outer2 = jnp.concatenate([low[2 * r :], below[2 * r :] - far[1]], axis=0).astype(BF16).astype(F32)
    edge_fill(p, blocks, tails, fill_low, 0, 0, 0)
    edge_fill(p, blocks, tails, outer2, 2, 5, 3)
    forward((0,), up_corners, up_count, target_ref[pl.ds(0, r), :], up_source)
    forward((3,), down_corners, down_count, target_ref[pl.ds(r + p.rows, r), :], down_source)
    lo = jnp.dot(own_t[pl.ds(LANES, 2 * LANES + p.tail), :], source[:, pl.ds(0, p.width)],
                 preferred_element_type=F32)
    hi = jnp.dot(jnp.concatenate([own_t[pl.ds(0, 2 * LANES), :], own_t[pl.ds(3 * LANES, p.tail), :]], axis=0),
                 source[:, pl.ds(p.width, p.width)], preferred_element_type=F32)
    ups = jnp.dot(up_t[...], up_source[...], preferred_element_type=F32)
    downs = jnp.dot(down_t[...], down_source[...], preferred_element_type=F32)

    def near_rows(b):
        if b < p.side - 1:
            at = b * r
            return [lo[at : at + r] + hi[at : at + r] + ups[at : at + r],
                    lo[LANES + at : LANES + at + r] + hi[LANES + at : LANES + at + r] + downs[at : at + r]]
        x, y = lo[2 * LANES :], hi[2 * LANES :]
        u, d = ups[LANES:], downs[LANES:]
        return [x[r : 2 * r] + y[:r] + u[2 * r : 3 * r], x[2 * r : 3 * r] + y[r : 2 * r] + d[:r]]

    out_ref[...] = own - STEP_RATE * gathered(near_rows)


def edge_fill(p, blocks, tails, value, which, block, tail):
    r = p.radius
    moved = [shifted(value, r - b) for b in range(p.side)]
    rows = slice(which * r, (which + 1) * r)
    for b in range(0, p.side - 1, 2):
        two = jnp.concatenate([moved[b][rows], moved[b + 1][rows]], axis=0)
        blocks[pl.ds(block * LANES + b * r, 2 * r), :] = two.astype(BF16)
    padded = jnp.concatenate([moved[p.side - 1], jnp.zeros((r, p.width), F32)], axis=0)
    tails[tail] = padded.astype(BF16)


def body(devices, mask, target, kernels, corner_weights, hotspots, counts):
    rows, width = mask.shape
    p = Plan(rows, width, kernels.shape[0], kernels.shape[1], kernels.shape[-1], hotspots.shape[1])
    assert rows == 2 * p.radius and p.radius == 8 and p.side == 17
    taps = jnp.transpose(kernels, (0, 2, 1, 3))
    vmem = pl.BlockSpec(memory_space=pltpu.VMEM)
    r = p.radius
    return pl.pallas_call(
        functools.partial(kernel, p, devices),
        out_shape=pltpu.VMEM((rows, width), F32),
        in_specs=[pl.BlockSpec(memory_space=pl.ANY)] * 6,
        out_specs=vmem,
        scratch_shapes=[
            pltpu.SMEM(hotspots.shape[::-1], hotspots.dtype),
            pltpu.SMEM(counts.shape, counts.dtype),
            pltpu.SMEM(corner_weights.shape, corner_weights.dtype),
            pltpu.VMEM((p.ext, width), target.dtype),
            pltpu.VMEM(taps.shape, taps.dtype),
            pltpu.VMEM((p.corners * p.channels, p.packed), F32),
            pltpu.VMEM((p.corners, p.slot_rows, p.depth), BF16),
            pltpu.VMEM((p.deep, p.mix), BF16),
            pltpu.VMEM((LANES + p.tail, p.mix), BF16),
            pltpu.VMEM((LANES + p.tail, p.mix), BF16),
            pltpu.VMEM((6 * LANES, width), BF16),
            pltpu.VMEM((4, p.tail, width), BF16),
            pltpu.VMEM((p.mix, 2 * width), BF16),
            pltpu.VMEM((p.mix, width), BF16),
            pltpu.VMEM((p.mix, width), BF16),
            pltpu.VMEM((p.ext, width), F32),
            pltpu.VMEM((p.ext, width), F32),
            pltpu.VMEM((2, 3 * r, width), F32),
            pltpu.VMEM((2, r, width), F32),
            pltpu.SemaphoreType.DMA((6,)),
            pltpu.SemaphoreType.DMA((4, 2)),
            pltpu.SemaphoreType.DMA((4, 2)),
        ],
        compiler_params=pltpu.CompilerParams(collective_id=0, has_side_effects=True),
        name="litho",
    )(hotspots.T, counts, corner_weights, mask, target, taps)


def solution(mesh):
    placed = (
        P(("strip", "row"), None),
        P(("strip", "row"), None),
        P(),
        P(),
        P("strip", None),
        P("strip"),
    )
    return jax.shard_map(
        functools.partial(body, mesh.shape["row"]), mesh=mesh, in_specs=placed,
        out_specs=P(("strip", "row"), None), check_vma=False
    )
```

```python
import functools

import jax
import jax.numpy as jnp
from jax import lax
from jax.experimental import pallas as pl
from jax.experimental.pallas import tpu as pltpu
from jax.sharding import PartitionSpec as P

STEEPNESS = 4.0
THRESHOLD = 0.8
STEP_RATE = 1.0
LANES = 128
MESH = pl.DeviceIdType.MESH
F32, BF16 = jnp.float32, jnp.bfloat16


def cdiv(a, b):
    return -(-a // b)


def round_up(a, b):
    return cdiv(a, b) * b


class Plan:
    def __init__(self, rows, width, corners, channels, side, slots):
        self.rows, self.width, self.corners, self.channels = rows, width, corners, channels
        self.side, self.slots = side, slots
        self.radius = side // 2
        self.ext = rows + 2 * self.radius
        self.tail = 4 * self.radius
        self.deep = 3 * LANES + self.tail
        self.depth = 4 * LANES
        self.lane_step = 32
        self.packed = cdiv(side * self.lane_step, LANES) * LANES
        self.slot_rows = channels * self.radius
        self.used = slots * self.slot_rows
        self.mix = round_up(self.used, 256)


def shifted(value, by):
    width = value.shape[1]
    if by == 0:
        return value
    moved = pltpu.roll(value, by % width, 1)
    column = lax.broadcasted_iota(jnp.int32, value.shape, 1)
    keep = column >= by if by > 0 else column < width + by
    return jnp.where(keep, moved, 0.0)


def kernel(p, devices, hot_hbm, count_hbm, weight_hbm, mask_hbm, target_hbm, taps_hbm, out_ref,
           hot_ref, count_ref, weight_ref, target_ref, taps, pack, base_ref, own_big, up_big, down_big,
           own_t, up_t, down_t, blocks, tails, source, up_source, down_source, partial, field, total,
           got_near, got_rest, got_far,
           load_sem, send_sem, recv_sem):
    me = lax.axis_index("row")
    r = p.radius
    has_up, has_down = me > 0, me < devices - 1
    has_up2, has_down2 = me > 1, me < devices - 2
    kinds = weight_hbm.shape[1]

    barrier = pltpu.get_barrier_semaphore()

    @pl.when(has_up)
    def _():
        pl.semaphore_signal(barrier, inc=1, device_id={"row": me - 1}, device_id_type=MESH)

    @pl.when(has_down)
    def _():
        pl.semaphore_signal(barrier, inc=1, device_id={"row": me + 1}, device_id_type=MESH)

    pairs = ((mask_hbm, field.at[pl.ds(r, p.rows)]), (target_hbm, target_ref.at[pl.ds(r, p.rows)]),
             (taps_hbm, taps), (hot_hbm, hot_ref), (count_hbm, count_ref), (weight_hbm, weight_ref))
    loads = [pltpu.make_async_copy(a, b, load_sem.at[k]) for k, (a, b) in enumerate(pairs)]
    for load in loads:
        load.start()

    def copies(stage, reach, up_src, down_src, above, below):
        up = pltpu.make_async_remote_copy(
            src_ref=up_src, dst_ref=below, send_sem=send_sem.at[stage, 0],
            recv_sem=recv_sem.at[stage, 0], device_id={"row": me - reach}, device_id_type=MESH)
        down = pltpu.make_async_remote_copy(
            src_ref=down_src, dst_ref=above, send_sem=send_sem.at[stage, 1],
            recv_sem=recv_sem.at[stage, 1], device_id={"row": me + reach}, device_id_type=MESH)
        return reach, up, down

    def start(pair):
        reach, up, down = pair

        @pl.when(me >= reach)
        def _():
            up.start()

        @pl.when(me < devices - reach)
        def _():
            down.start()

    def finish(pair):
        reach, up, down = pair

        @pl.when(me >= reach)
        def _():
            up.wait_send()
            down.wait_recv()

        @pl.when(me < devices - reach)
        def _():
            down.wait_send()
            up.wait_recv()

    def clear(ref, where):
        ref[where] = jnp.zeros(ref.at[where].shape, ref.dtype)

    spot = lax.broadcasted_iota(jnp.int32, (1, p.depth), 1)
    in_tail = spot >= 3 * LANES
    inside = spot & (LANES - 1)
    tap_row = jnp.where(in_tail, inside, (spot // LANES) * r + (inside & (r - 1)))
    tap_col = jnp.where(in_tail, p.side - 1, inside // r)
    wanted = jnp.where(tap_row < p.side, tap_row * p.lane_step + tap_col, -1)
    place = (lax.broadcasted_iota(jnp.int32, (p.packed, p.depth), 0) == wanted).astype(F32).astype(BF16)

    inner = has_up & has_down

    loads[0].wait()

    @pl.when(inner)
    def _():
        pl.semaphore_wait(barrier, 2)

    @pl.when(jnp.logical_not(inner))
    def _():
        pl.semaphore_wait(barrier, 1)

    first = copies(0, 1, field.at[pl.ds(r, r)], field.at[pl.ds(p.rows, r)],
                   field.at[pl.ds(0, r)], field.at[pl.ds(r + p.rows, r)])
    start(first)
    aims = copies(1, 1, target_hbm.at[pl.ds(0, r)], target_hbm.at[pl.ds(p.rows - r, r)],
                  target_ref.at[pl.ds(0, r)], target_ref.at[pl.ds(r + p.rows, r)])
    start(aims)

    @pl.when(jnp.logical_not(has_up))
    def _():
        clear(field, pl.ds(0, r))
        clear(target_ref, pl.ds(0, r))
        clear(got_near, 0)
        clear(got_rest, 0)

    @pl.when(jnp.logical_not(has_down))
    def _():
        clear(field, pl.ds(r + p.rows, r))
        clear(target_ref, pl.ds(r + p.rows, r))
        clear(got_near, 1)
        clear(got_rest, 1)

    @pl.when(jnp.logical_not(has_up2))
    def _():
        clear(got_far, 0)

    @pl.when(jnp.logical_not(has_down2))
    def _():
        clear(got_far, 1)

    pack[...] = jnp.zeros(pack.shape, F32)
    for load in loads[1:]:
        load.wait()

    for c in range(p.corners):
        for a in range(p.side):
            pack[pl.ds(c * p.channels, p.channels), pl.ds(a * p.lane_step, p.side)] = (
                taps[c, a].astype(F32))
    base = jnp.dot(pack[...].astype(BF16), place, preferred_element_type=F32)
    lane = lax.broadcasted_iota(jnp.int32, (1, r, LANES), 2)
    phase = lax.broadcasted_iota(jnp.int32, (1, r, LANES), 1)
    straight = (lane & (r - 1)) + phase < r
    for c in range(p.corners):
        span = slice(c * p.channels, (c + 1) * p.channels)
        base_ref[c, :, pl.ds(0, p.depth)] = base[span]
        for q in range(2):
            base_ref[c, :, pl.ds((4 + q) * LANES, LANES)] = pltpu.roll(
                base[span, q * LANES : (q + 1) * LANES], LANES - r, 1)

    def spread_out(chosen, into):
        def wide(c, q):
            part = base_ref[c, :, pl.ds(q * LANES, LANES)]
            return jnp.broadcast_to(part[:, None, :], (p.channels, r, LANES))

        for s in range(p.slots):
            for q in range(4):
                here = wide(chosen[s], q)
                if q < 3:
                    here = jnp.where(straight, here, wide(chosen[s], q + 3) if q else 0.0)
                turned = pltpu.roll(here, 0, 2, stride=1, stride_axis=1)
                into[pl.ds(s * p.slot_rows, p.slot_rows), pl.ds(q * LANES, LANES)] = (
                    turned.reshape(p.slot_rows, LANES).astype(BF16))
        if p.mix > p.used:
            clear(into, pl.ds(p.used, p.mix - p.used))

    up_tile, down_tile = jnp.maximum(me - 1, 0), jnp.minimum(me + 1, devices - 1)
    corners = [hot_ref[s, me] for s in range(p.slots)]
    up_corners = [hot_ref[s, up_tile] for s in range(p.slots)]
    down_corners = [hot_ref[s, down_tile] for s in range(p.slots)]
    count = count_ref[me]
    up_count = jnp.where(has_up, count_ref[up_tile], 0)
    down_count = jnp.where(has_down, count_ref[down_tile], 0)

    def turn(whole, quarters, into):
        for q in range(p.mix // 256):
            for n, quarter in enumerate(quarters):
                tall = p.tail if quarter == 3 else LANES
                turned = whole[pl.ds(q * 256, 256), pl.ds(quarter * LANES, LANES)].astype(F32).T
                into[pl.ds(n * LANES, tall), pl.ds(q * 256, 256)] = turned[:tall].astype(BF16)

    for ref in (source, up_source, down_source):
        if p.mix > p.used:
            clear(ref, pl.ds(p.used, p.mix - p.used))
    spread_out(corners, own_big)
    turn(own_big, (0, 1, 2, 3), own_t)

    def lay(value, which):
        for b in range(0, p.side - 1, 2):
            left, right = shifted(value, r - b), shifted(value, r - b - 1)
            for n, i in enumerate(which):
                rows = slice(n * r, (n + 1) * r)
                blocks[pl.ds(i * LANES + b * r, 2 * r), :] = (
                    jnp.concatenate([left[rows], right[rows]], axis=0).astype(BF16))

    def lay_tails(value, which):
        last = shifted(value, r - p.side + 1)
        for n, g in enumerate(which):
            padded = jnp.concatenate([last[n * r : (n + 3) * r], jnp.zeros((r, p.width), F32)], axis=0)
            tails[g] = padded.astype(BF16)

    def patch(g):
        return jnp.concatenate([blocks[pl.ds(g * LANES, 3 * LANES), :], tails[g]], axis=0)

    def excite(s, image, n, chosen, limit, aim, into):
        image = image.reshape(p.channels, r, n)
        weights = [weight_ref[chosen[s], k] for k in range(kinds)]
        intensity = jnp.zeros((r, n), F32)
        for k in range(kinds):
            both_parts = image[k] * image[k] + image[k + kinds] * image[k + kinds]
            intensity = intensity + weights[k] * both_parts
        resist = jax.nn.sigmoid(STEEPNESS * (intensity - THRESHOLD))
        slope = 2.0 * (resist - aim) * STEEPNESS * resist * (1.0 - resist)
        slope = jnp.where(s < limit, slope, 0.0)
        scaled = [(2.0 * weights[k]) * slope for k in range(kinds)]
        sent = jnp.stack([scaled[j % kinds] * image[j] for j in range(p.channels)])
        into[pl.ds(s * p.slot_rows, p.slot_rows), :] = sent.reshape(p.slot_rows, n).astype(BF16)

    def forward(groups, whole, chosen, limit, aim, into):
        patches = jnp.concatenate([patch(g) for g in groups], axis=1)
        for s in range(p.slots):
            image = jnp.dot(whole[pl.ds(s * p.slot_rows, p.slot_rows), pl.ds(0, p.deep)], patches,
                            preferred_element_type=F32)
            excite(s, image, len(groups) * p.width, chosen, limit, aim, into)

    def forward_own_rows():
        inner_blocks = blocks[pl.ds(2 * LANES, 2 * LANES), :]
        for g in range(2):
            partial[:, pl.ds(g * p.width, p.width)] = jnp.dot(
                own_big[pl.ds(0, p.used), pl.ds((1 - g) * LANES, 2 * LANES)], inner_blocks,
                preferred_element_type=F32)

    def forward_halo_rows(aim):
        for s in range(p.slots):
            rows = pl.ds(s * p.slot_rows, p.slot_rows)
            both = []
            for g in range(2):
                left = jnp.concatenate([own_big[rows, pl.ds(2 * g * LANES, LANES)],
                                        own_big[rows, pl.ds(3 * LANES, p.tail)]], axis=1)
                right = jnp.concatenate([blocks[pl.ds((1 + 3 * g) * LANES, LANES), :], tails[1 + g]], axis=0)
                both.append(jnp.dot(left, right, preferred_element_type=F32))
            image = partial[rows, :] + jnp.concatenate(both, axis=1)
            excite(s, image, 2 * p.width, corners, count, aim, source)

    def gathered(rows_of):
        sums = 0.0
        for b in range(p.side):
            sums = sums + shifted(jnp.concatenate(rows_of(b), axis=0), b - r)
        return sums

    def third(value, w, b, base=0):
        at = (w - base) * LANES + b * r if b < p.side - 1 else (3 - base) * LANES + w * r
        return value[at : at + r]

    lay(field[pl.ds(r, p.rows), :].astype(BF16).astype(F32), (2, 3))
    forward_own_rows()
    finish(first)
    aim = jnp.concatenate([target_ref[pl.ds((g + 1) * r, r), :] for g in range(2)], axis=1)
    low = field[...].astype(BF16).astype(F32)
    lay(jnp.concatenate([low[:r], low[r + p.rows :]], axis=0), (1, 4))
    lay_tails(low, (1, 2))
    forward_halo_rows(aim)
    spread = [jnp.dot(own_t[...], source[:, pl.ds(g * p.width, p.width)], preferred_element_type=F32)
              for g in range(2)]
    lo, hi = spread
    gradient = STEP_RATE * gathered(lambda b: [
        third(lo, 0, b), third(lo, 1, b) + third(hi, 0, b), third(lo, 2, b) + third(hi, 1, b),
        third(hi, 2, b)])
    total[pl.ds(0, r), :] = gradient[:r]
    total[pl.ds(r, p.rows), :] = field[pl.ds(r, p.rows), :] - gradient[r : r + p.rows]
    total[pl.ds(r + p.rows, r), :] = gradient[r + p.rows :]
    near = copies(2, 1, total.at[pl.ds(0, 2 * r)], total.at[pl.ds(2 * r, 2 * r)], got_near.at[0], got_near.at[1])
    start(near)
    rest = copies(3, 1, total.at[pl.ds(2 * r, r)], total.at[pl.ds(r, r)], got_rest.at[0], got_rest.at[1])
    start(rest)
    beyond = copies(4, 2, total.at[pl.ds(0, r)], total.at[pl.ds(3 * r, r)], got_far.at[0], got_far.at[1])
    start(beyond)

    forward((1, 2), own_big, corners, count, aim, source)
    spread_out(up_corners, up_big)
    spread_out(down_corners, down_big)
    turn(up_big, (2, 3), up_t)
    turn(down_big, (0, 3), down_t)
    finish(aims)
    finish(near)
    above, below = got_near[0], got_near[1]
    upper = jnp.where(has_up, total[pl.ds(0, r), :], 0.0)
    lower = jnp.where(has_down, total[pl.ds(3 * r, r), :], 0.0)
    own = total[pl.ds(r, p.rows), :] - jnp.concatenate([above[r:], below[:r]], axis=0)
    after = jnp.concatenate([above[:r] - upper, own, below[r:] - lower], axis=0)
    low = after.astype(BF16).astype(F32)
    lay(low, (1, 2, 3, 4))
    lay_tails(low, (1, 2))
    forward((1, 2), own_big, corners, count, aim, source)
    finish(rest)
    finish(beyond)
    outer = jnp.concatenate([got_rest[0] - got_far[0], got_rest[1] - got_far[1]], axis=0)
    outer = outer.astype(BF16).astype(F32)
    lay(outer, (0, 5))
    lay_tails(jnp.concatenate([outer[:r], low[: 2 * r]], axis=0), (0,))
    lay_tails(jnp.concatenate([low[2 * r :], outer[r:]], axis=0), (3,))
    forward((0,), up_big, up_corners, up_count, target_ref[pl.ds(0, r), :], up_source)
    forward((3,), down_big, down_corners, down_count, target_ref[pl.ds(r + p.rows, r), :], down_source)
    lo = jnp.dot(own_t[pl.ds(LANES, 2 * LANES + p.tail), :], source[:, pl.ds(0, p.width)],
                 preferred_element_type=F32)
    hi = jnp.dot(jnp.concatenate([own_t[pl.ds(0, 2 * LANES), :], own_t[pl.ds(3 * LANES, p.tail), :]], axis=0),
                 source[:, pl.ds(p.width, p.width)], preferred_element_type=F32)
    ups = jnp.dot(up_t[...], up_source[...], preferred_element_type=F32)
    downs = jnp.dot(down_t[...], down_source[...], preferred_element_type=F32)

    def near_rows(b):
        if b < p.side - 1:
            at = b * r
            return [lo[at : at + r] + hi[at : at + r] + ups[at : at + r],
                    lo[LANES + at : LANES + at + r] + hi[LANES + at : LANES + at + r] + downs[at : at + r]]
        x, y = lo[2 * LANES :], hi[2 * LANES :]
        u, d = ups[LANES:], downs[LANES:]
        return [x[r : 2 * r] + y[:r] + u[2 * r : 3 * r], x[2 * r : 3 * r] + y[r : 2 * r] + d[:r]]

    out_ref[...] = own - STEP_RATE * gathered(near_rows)


def body(devices, mask, target, kernels, corner_weights, hotspots, counts):
    rows, width = mask.shape
    p = Plan(rows, width, kernels.shape[0], kernels.shape[1], kernels.shape[-1], hotspots.shape[1])
    assert rows == 2 * p.radius and p.radius == 8 and p.side == 17
    taps = jnp.transpose(kernels, (0, 2, 1, 3))
    vmem = pl.BlockSpec(memory_space=pltpu.VMEM)
    r = p.radius
    return pl.pallas_call(
        functools.partial(kernel, p, devices),
        out_shape=pltpu.VMEM((rows, width), F32),
        in_specs=[pl.BlockSpec(memory_space=pl.ANY)] * 6,
        out_specs=vmem,
        scratch_shapes=[
            pltpu.SMEM(hotspots.shape[::-1], hotspots.dtype),
            pltpu.SMEM(counts.shape, counts.dtype),
            pltpu.SMEM(corner_weights.shape, corner_weights.dtype),
            pltpu.VMEM((p.ext, width), target.dtype),
            pltpu.VMEM(taps.shape, taps.dtype),
            pltpu.VMEM((p.corners * p.channels, p.packed), F32),
            pltpu.VMEM((p.corners, p.channels, 6 * LANES), F32),
            pltpu.VMEM((p.mix, p.depth), BF16),
            pltpu.VMEM((p.mix, p.depth), BF16),
            pltpu.VMEM((p.mix, p.depth), BF16),
            pltpu.VMEM((p.deep, p.mix), BF16),
            pltpu.VMEM((LANES + p.tail, p.mix), BF16),
            pltpu.VMEM((LANES + p.tail, p.mix), BF16),
            pltpu.VMEM((6 * LANES, width), BF16),
            pltpu.VMEM((4, p.tail, width), BF16),
            pltpu.VMEM((p.mix, 2 * width), BF16),
            pltpu.VMEM((p.mix, width), BF16),
            pltpu.VMEM((p.mix, width), BF16),
            pltpu.VMEM((p.used, 2 * width), F32),
            pltpu.VMEM((p.ext, width), F32),
            pltpu.VMEM((p.ext, width), F32),
            pltpu.VMEM((2, 2 * r, width), F32),
            pltpu.VMEM((2, r, width), F32),
            pltpu.VMEM((2, r, width), F32),
            pltpu.SemaphoreType.DMA((6,)),
            pltpu.SemaphoreType.DMA((5, 2)),
            pltpu.SemaphoreType.DMA((5, 2)),
        ],
        compiler_params=pltpu.CompilerParams(collective_id=0, has_side_effects=True),
        name="litho",
    )(hotspots.T, counts, corner_weights, mask, target, taps)


def solution(mesh):
    placed = (
        P(("strip", "row"), None),
        P(("strip", "row"), None),
        P(),
        P(),
        P("strip", None),
        P("strip"),
    )
    return jax.shard_map(
        functools.partial(body, mesh.shape["row"]), mesh=mesh, in_specs=placed,
        out_specs=P(("strip", "row"), None), check_vma=False
    )
```

```python
import functools

import jax
import jax.numpy as jnp
from jax import lax
from jax.experimental import pallas as pl
from jax.experimental.pallas import tpu as pltpu
from jax.sharding import PartitionSpec as P

STEEPNESS = 4.0
THRESHOLD = 0.8
STEP_RATE = 1.0
LANES = 128
MESH = pl.DeviceIdType.MESH
F32, BF16 = jnp.float32, jnp.bfloat16


def cdiv(a, b):
    return -(-a // b)


def round_up(a, b):
    return cdiv(a, b) * b


class Plan:
    def __init__(self, rows, width, corners, channels, side, slots):
        self.rows, self.width, self.corners, self.channels = rows, width, corners, channels
        self.side, self.slots = side, slots
        self.radius = side // 2
        self.ext = rows + 2 * self.radius
        self.tail = 4 * self.radius
        self.deep = 3 * LANES + self.tail
        self.depth = 4 * LANES
        self.lane_step = 32
        self.packed = cdiv(side * self.lane_step, LANES) * LANES
        self.slot_rows = channels * self.radius
        self.used = slots * self.slot_rows
        self.mix = round_up(self.used, 256)


def shifted(value, by):
    width = value.shape[1]
    if by == 0:
        return value
    moved = pltpu.roll(value, by % width, 1)
    column = lax.broadcasted_iota(jnp.int32, value.shape, 1)
    keep = column >= by if by > 0 else column < width + by
    return jnp.where(keep, moved, 0.0)


def kernel(p, devices, hot_hbm, count_hbm, weight_hbm, mask_hbm, target_hbm, taps_hbm, out_ref,
           hot_ref, count_ref, weight_ref, target_ref, taps, pack, base_ref, own_big, up_big, down_big,
           own_t, up_t, down_t, blocks, tails, source, up_source, down_source, partial, field, total,
           got_near, got_rest, got_far,
           load_sem, send_sem, recv_sem):
    me = lax.axis_index("row")
    r = p.radius
    has_up, has_down = me > 0, me < devices - 1
    has_up2, has_down2 = me > 1, me < devices - 2
    kinds = weight_hbm.shape[1]

    barrier = pltpu.get_barrier_semaphore()

    @pl.when(has_up)
    def _():
        pl.semaphore_signal(barrier, inc=1, device_id={"row": me - 1}, device_id_type=MESH)

    @pl.when(has_down)
    def _():
        pl.semaphore_signal(barrier, inc=1, device_id={"row": me + 1}, device_id_type=MESH)

    pairs = ((mask_hbm, field.at[pl.ds(r, p.rows)]), (target_hbm, target_ref.at[pl.ds(r, p.rows)]),
             (hot_hbm, hot_ref), (count_hbm, count_ref), (weight_hbm, weight_ref), (taps_hbm, taps))
    loads = [pltpu.make_async_copy(a, b, load_sem.at[k]) for k, (a, b) in enumerate(pairs)]
    for load in loads:
        load.start()

    def copies(stage, reach, up_src, down_src, above, below):
        up = pltpu.make_async_remote_copy(
            src_ref=up_src, dst_ref=below, send_sem=send_sem.at[stage, 0],
            recv_sem=recv_sem.at[stage, 0], device_id={"row": me - reach}, device_id_type=MESH)
        down = pltpu.make_async_remote_copy(
            src_ref=down_src, dst_ref=above, send_sem=send_sem.at[stage, 1],
            recv_sem=recv_sem.at[stage, 1], device_id={"row": me + reach}, device_id_type=MESH)
        return reach, up, down

    def start(pair):
        reach, up, down = pair

        @pl.when(me >= reach)
        def _():
            up.start()

        @pl.when(me < devices - reach)
        def _():
            down.start()

    def finish(pair):
        reach, up, down = pair

        @pl.when(me >= reach)
        def _():
            up.wait_send()
            down.wait_recv()

        @pl.when(me < devices - reach)
        def _():
            down.wait_send()
            up.wait_recv()

    def clear(ref, where):
        ref[where] = jnp.zeros(ref.at[where].shape, ref.dtype)

    spot = lax.broadcasted_iota(jnp.int32, (1, p.depth), 1)
    in_tail = spot >= 3 * LANES
    inside = spot & (LANES - 1)
    tap_row = jnp.where(in_tail, inside, (spot // LANES) * r + (inside & (r - 1)))
    tap_col = jnp.where(in_tail, p.side - 1, inside // r)
    wanted = jnp.where(tap_row < p.side, tap_row * p.lane_step + tap_col, -1)
    place = (lax.broadcasted_iota(jnp.int32, (p.packed, p.depth), 0) == wanted).astype(F32).astype(BF16)

    inner = has_up & has_down

    loads[0].wait()

    @pl.when(inner)
    def _():
        pl.semaphore_wait(barrier, 2)

    @pl.when(jnp.logical_not(inner))
    def _():
        pl.semaphore_wait(barrier, 1)

    first = copies(0, 1, field.at[pl.ds(r, r)], field.at[pl.ds(p.rows, r)],
                   field.at[pl.ds(0, r)], field.at[pl.ds(r + p.rows, r)])
    start(first)
    aims = copies(1, 1, target_hbm.at[pl.ds(0, r)], target_hbm.at[pl.ds(p.rows - r, r)],
                  target_ref.at[pl.ds(0, r)], target_ref.at[pl.ds(r + p.rows, r)])
    start(aims)

    @pl.when(jnp.logical_not(has_up))
    def _():
        clear(field, pl.ds(0, r))
        clear(target_ref, pl.ds(0, r))
        clear(got_near, 0)
        clear(got_rest, 0)

    @pl.when(jnp.logical_not(has_down))
    def _():
        clear(field, pl.ds(r + p.rows, r))
        clear(target_ref, pl.ds(r + p.rows, r))
        clear(got_near, 1)
        clear(got_rest, 1)

    @pl.when(jnp.logical_not(has_up2))
    def _():
        clear(got_far, 0)

    @pl.when(jnp.logical_not(has_down2))
    def _():
        clear(got_far, 1)

    pack[...] = jnp.zeros(pack.shape, F32)
    for load in loads[1:]:
        load.wait()

    for c in range(p.corners):
        for a in range(p.side):
            pack[pl.ds(c * p.channels, p.channels), pl.ds(a * p.lane_step, p.side)] = (
                taps[c, a].astype(F32))
    base = jnp.dot(pack[...].astype(BF16), place, preferred_element_type=F32)
    lane = lax.broadcasted_iota(jnp.int32, (1, r, LANES), 2)
    phase = lax.broadcasted_iota(jnp.int32, (1, r, LANES), 1)
    straight = (lane & (r - 1)) + phase < r
    for c in range(p.corners):
        span = slice(c * p.channels, (c + 1) * p.channels)
        base_ref[c, :, pl.ds(0, p.depth)] = base[span]
        for q in range(2):
            base_ref[c, :, pl.ds((4 + q) * LANES, LANES)] = pltpu.roll(
                base[span, q * LANES : (q + 1) * LANES], LANES - r, 1)

    def spread_out(chosen, into):
        def wide(c, q):
            part = base_ref[c, :, pl.ds(q * LANES, LANES)]
            return jnp.broadcast_to(part[:, None, :], (p.channels, r, LANES))

        for s in range(p.slots):
            for q in range(4):
                here = wide(chosen[s], q)
                if q < 3:
                    here = jnp.where(straight, here, wide(chosen[s], q + 3) if q else 0.0)
                turned = pltpu.roll(here, 0, 2, stride=1, stride_axis=1)
                into[pl.ds(s * p.slot_rows, p.slot_rows), pl.ds(q * LANES, LANES)] = (
                    turned.reshape(p.slot_rows, LANES).astype(BF16))
        if p.mix > p.used:
            clear(into, pl.ds(p.used, p.mix - p.used))

    up_tile, down_tile = jnp.maximum(me - 1, 0), jnp.minimum(me + 1, devices - 1)
    corners = [hot_ref[s, me] for s in range(p.slots)]
    up_corners = [hot_ref[s, up_tile] for s in range(p.slots)]
    down_corners = [hot_ref[s, down_tile] for s in range(p.slots)]
    count = count_ref[me]
    up_count = jnp.where(has_up, count_ref[up_tile], 0)
    down_count = jnp.where(has_down, count_ref[down_tile], 0)

    def turn(whole, quarters, into):
        for q in range(p.mix // 256):
            for n, quarter in enumerate(quarters):
                tall = p.tail if quarter == 3 else LANES
                turned = whole[pl.ds(q * 256, 256), pl.ds(quarter * LANES, LANES)].astype(F32).T
                into[pl.ds(n * LANES, tall), pl.ds(q * 256, 256)] = turned[:tall].astype(BF16)

    for ref in (source, up_source, down_source):
        if p.mix > p.used:
            clear(ref, pl.ds(p.used, p.mix - p.used))
    spread_out(corners, own_big)
    turn(own_big, (0, 1, 2, 3), own_t)

    def lay(value, which):
        for b in range(0, p.side - 1, 2):
            left, right = shifted(value, r - b), shifted(value, r - b - 1)
            for n, i in enumerate(which):
                rows = slice(n * r, (n + 1) * r)
                blocks[pl.ds(i * LANES + b * r, 2 * r), :] = (
                    jnp.concatenate([left[rows], right[rows]], axis=0).astype(BF16))

    def lay_tails(value, which):
        last = shifted(value, r - p.side + 1)
        for n, g in enumerate(which):
            padded = jnp.concatenate([last[n * r : (n + 3) * r], jnp.zeros((r, p.width), F32)], axis=0)
            tails[g] = padded.astype(BF16)

    def patch(g):
        return jnp.concatenate([blocks[pl.ds(g * LANES, 3 * LANES), :], tails[g]], axis=0)

    def excite(s, image, n, chosen, limit, aim, into):
        image = image.reshape(p.channels, r, n)
        weights = [weight_ref[chosen[s], k] for k in range(kinds)]
        intensity = jnp.zeros((r, n), F32)
        for k in range(kinds):
            both_parts = image[k] * image[k] + image[k + kinds] * image[k + kinds]
            intensity = intensity + weights[k] * both_parts
        resist = jax.nn.sigmoid(STEEPNESS * (intensity - THRESHOLD))
        slope = 2.0 * (resist - aim) * STEEPNESS * resist * (1.0 - resist)
        slope = jnp.where(s < limit, slope, 0.0)
        scaled = [(2.0 * weights[k]) * slope for k in range(kinds)]
        sent = jnp.stack([scaled[j % kinds] * image[j] for j in range(p.channels)])
        into[pl.ds(s * p.slot_rows, p.slot_rows), :] = sent.reshape(p.slot_rows, n).astype(BF16)

    def forward(groups, whole, chosen, limit, aim, into):
        patches = jnp.concatenate([patch(g) for g in groups], axis=1)
        for s in range(p.slots):
            image = jnp.dot(whole[pl.ds(s * p.slot_rows, p.slot_rows), pl.ds(0, p.deep)], patches,
                            preferred_element_type=F32)
            excite(s, image, len(groups) * p.width, chosen, limit, aim, into)

    def forward_own_rows():
        inner_blocks = blocks[pl.ds(2 * LANES, 2 * LANES), :]
        for g in range(2):
            partial[:, pl.ds(g * p.width, p.width)] = jnp.dot(
                own_big[pl.ds(0, p.used), pl.ds((1 - g) * LANES, 2 * LANES)], inner_blocks,
                preferred_element_type=F32)

    def forward_halo_rows(aim):
        for s in range(p.slots):
            rows = pl.ds(s * p.slot_rows, p.slot_rows)
            both = []
            for g in range(2):
                left = jnp.concatenate([own_big[rows, pl.ds(2 * g * LANES, LANES)],
                                        own_big[rows, pl.ds(3 * LANES, p.tail)]], axis=1)
                right = jnp.concatenate([blocks[pl.ds((1 + 3 * g) * LANES, LANES), :], tails[1 + g]], axis=0)
                both.append(jnp.dot(left, right, preferred_element_type=F32))
            image = partial[rows, :] + jnp.concatenate(both, axis=1)
            excite(s, image, 2 * p.width, corners, count, aim, source)

    def gathered(rows_of):
        sums = 0.0
        for b in range(p.side):
            sums = sums + shifted(jnp.concatenate(rows_of(b), axis=0), b - r)
        return sums

    def third(value, w, b, base=0):
        at = (w - base) * LANES + b * r if b < p.side - 1 else (3 - base) * LANES + w * r
        return value[at : at + r]

    lay(field[pl.ds(r, p.rows), :].astype(BF16).astype(F32), (2, 3))
    forward_own_rows()
    finish(first)
    aim = jnp.concatenate([target_ref[pl.ds((g + 1) * r, r), :] for g in range(2)], axis=1)
    low = field[...].astype(BF16).astype(F32)
    lay(jnp.concatenate([low[:r], low[r + p.rows :]], axis=0), (1, 4))
    lay_tails(low, (1, 2))
    forward_halo_rows(aim)
    spread = [jnp.dot(own_t[...], source[:, pl.ds(g * p.width, p.width)], preferred_element_type=F32)
              for g in range(2)]
    lo, hi = spread
    gradient = STEP_RATE * gathered(lambda b: [
        third(lo, 0, b), third(lo, 1, b) + third(hi, 0, b), third(lo, 2, b) + third(hi, 1, b),
        third(hi, 2, b)])
    total[pl.ds(0, r), :] = gradient[:r]
    total[pl.ds(r, p.rows), :] = field[pl.ds(r, p.rows), :] - gradient[r : r + p.rows]
    total[pl.ds(r + p.rows, r), :] = gradient[r + p.rows :]
    near = copies(2, 1, total.at[pl.ds(0, 2 * r)], total.at[pl.ds(2 * r, 2 * r)], got_near.at[0], got_near.at[1])
    start(near)
    rest = copies(3, 1, total.at[pl.ds(2 * r, r)], total.at[pl.ds(r, r)], got_rest.at[0], got_rest.at[1])
    start(rest)
    beyond = copies(4, 2, total.at[pl.ds(0, r)], total.at[pl.ds(3 * r, r)], got_far.at[0], got_far.at[1])
    start(beyond)

    forward((1, 2), own_big, corners, count, aim, source)
    spread_out(up_corners, up_big)
    spread_out(down_corners, down_big)
    turn(up_big, (2, 3), up_t)
    turn(down_big, (0, 3), down_t)
    finish(aims)
    finish(near)
    above, below = got_near[0], got_near[1]
    upper = jnp.where(has_up, total[pl.ds(0, r), :], 0.0)
    lower = jnp.where(has_down, total[pl.ds(3 * r, r), :], 0.0)
    own = total[pl.ds(r, p.rows), :] - jnp.concatenate([above[r:], below[:r]], axis=0)
    after = jnp.concatenate([above[:r] - upper, own, below[r:] - lower], axis=0)
    low = after.astype(BF16).astype(F32)
    lay(low, (1, 2, 3, 4))
    lay_tails(low, (1, 2))
    forward((1, 2), own_big, corners, count, aim, source)
    finish(rest)
    finish(beyond)
    outer = jnp.concatenate([got_rest[0] - got_far[0], got_rest[1] - got_far[1]], axis=0)
    outer = outer.astype(BF16).astype(F32)
    lay(outer, (0, 5))
    lay_tails(jnp.concatenate([outer[:r], low[: 2 * r]], axis=0), (0,))
    lay_tails(jnp.concatenate([low[2 * r :], outer[r:]], axis=0), (3,))
    forward((0,), up_big, up_corners, up_count, target_ref[pl.ds(0, r), :], up_source)
    forward((3,), down_big, down_corners, down_count, target_ref[pl.ds(r + p.rows, r), :], down_source)
    lo = jnp.dot(own_t[pl.ds(LANES, 2 * LANES + p.tail), :], source[:, pl.ds(0, p.width)],
                 preferred_element_type=F32)
    hi = jnp.dot(jnp.concatenate([own_t[pl.ds(0, 2 * LANES), :], own_t[pl.ds(3 * LANES, p.tail), :]], axis=0),
                 source[:, pl.ds(p.width, p.width)], preferred_element_type=F32)
    ups = jnp.dot(up_t[...], up_source[...], preferred_element_type=F32)
    downs = jnp.dot(down_t[...], down_source[...], preferred_element_type=F32)

    def near_rows(b):
        if b < p.side - 1:
            at = b * r
            return [lo[at : at + r] + hi[at : at + r] + ups[at : at + r],
                    lo[LANES + at : LANES + at + r] + hi[LANES + at : LANES + at + r] + downs[at : at + r]]
        x, y = lo[2 * LANES :], hi[2 * LANES :]
        u, d = ups[LANES:], downs[LANES:]
        return [x[r : 2 * r] + y[:r] + u[2 * r : 3 * r], x[2 * r : 3 * r] + y[r : 2 * r] + d[:r]]

    out_ref[...] = own - STEP_RATE * gathered(near_rows)


def body(devices, mask, target, kernels, corner_weights, hotspots, counts):
    rows, width = mask.shape
    p = Plan(rows, width, kernels.shape[0], kernels.shape[1], kernels.shape[-1], hotspots.shape[1])
    assert rows == 2 * p.radius and p.radius == 8 and p.side == 17
    taps = jnp.transpose(kernels, (0, 2, 1, 3))
    vmem = pl.BlockSpec(memory_space=pltpu.VMEM)
    r = p.radius
    return pl.pallas_call(
        functools.partial(kernel, p, devices),
        out_shape=pltpu.VMEM((rows, width), F32),
        in_specs=[pl.BlockSpec(memory_space=pl.ANY)] * 6,
        out_specs=vmem,
        scratch_shapes=[
            pltpu.SMEM(hotspots.shape[::-1], hotspots.dtype),
            pltpu.SMEM(counts.shape, counts.dtype),
            pltpu.SMEM(corner_weights.shape, corner_weights.dtype),
            pltpu.VMEM((p.ext, width), target.dtype),
            pltpu.VMEM(taps.shape, taps.dtype),
            pltpu.VMEM((p.corners * p.channels, p.packed), F32),
            pltpu.VMEM((p.corners, p.channels, 6 * LANES), F32),
            pltpu.VMEM((p.mix, p.depth), BF16),
            pltpu.VMEM((p.mix, p.depth), BF16),
            pltpu.VMEM((p.mix, p.depth), BF16),
            pltpu.VMEM((p.deep, p.mix), BF16),
            pltpu.VMEM((LANES + p.tail, p.mix), BF16),
            pltpu.VMEM((LANES + p.tail, p.mix), BF16),
            pltpu.VMEM((6 * LANES, width), BF16),
            pltpu.VMEM((4, p.tail, width), BF16),
            pltpu.VMEM((p.mix, 2 * width), BF16),
            pltpu.VMEM((p.mix, width), BF16),
            pltpu.VMEM((p.mix, width), BF16),
            pltpu.VMEM((p.used, 2 * width), F32),
            pltpu.VMEM((p.ext, width), F32),
            pltpu.VMEM((p.ext, width), F32),
            pltpu.VMEM((2, 2 * r, width), F32),
            pltpu.VMEM((2, r, width), F32),
            pltpu.VMEM((2, r, width), F32),
            pltpu.SemaphoreType.DMA((6,)),
            pltpu.SemaphoreType.DMA((5, 2)),
            pltpu.SemaphoreType.DMA((5, 2)),
        ],
        compiler_params=pltpu.CompilerParams(collective_id=0, has_side_effects=True),
        name="litho",
    )(hotspots.T, counts, corner_weights, mask, target, taps)


def solution(mesh):
    placed = (
        P(("strip", "row"), None),
        P(("strip", "row"), None),
        P(),
        P(),
        P("strip", None),
        P("strip"),
    )
    return jax.shard_map(
        functools.partial(body, mesh.shape["row"]), mesh=mesh, in_specs=placed,
        out_specs=P(("strip", "row"), None), check_vma=False
    )
```

```python
import functools

import jax
import jax.numpy as jnp
from jax import lax
from jax.experimental import pallas as pl
from jax.experimental.pallas import tpu as pltpu
from jax.sharding import PartitionSpec as P

STEEPNESS = 4.0
THRESHOLD = 0.8
STEP_RATE = 1.0
LANES = 128
MESH = pl.DeviceIdType.MESH
F32, BF16 = jnp.float32, jnp.bfloat16


def cdiv(a, b):
    return -(-a // b)


def round_up(a, b):
    return cdiv(a, b) * b


class Plan:
    def __init__(self, rows, width, corners, channels, side, slots):
        self.rows, self.width, self.corners, self.channels = rows, width, corners, channels
        self.side, self.slots = side, slots
        self.radius = side // 2
        self.ext = rows + 2 * self.radius
        self.tail = 4 * self.radius
        self.deep = 3 * LANES + self.tail
        self.depth = 4 * LANES
        self.lane_step = 32
        self.packed = cdiv(side * self.lane_step, LANES) * LANES
        self.slot_rows = channels * self.radius
        self.used = slots * self.slot_rows
        self.mix = round_up(self.used, 256)


def shifted(value, by):
    width = value.shape[1]
    if by == 0:
        return value
    moved = pltpu.roll(value, by % width, 1)
    column = lax.broadcasted_iota(jnp.int32, value.shape, 1)
    keep = column >= by if by > 0 else column < width + by
    return jnp.where(keep, moved, 0.0)


def kernel(p, devices, hot_hbm, count_hbm, weight_hbm, mask_hbm, target_hbm, taps_hbm, out_ref,
           hot_ref, count_ref, weight_ref, target_ref, taps, pack, base_ref, own_big, up_big, down_big,
           own_t, up_t, down_t, blocks, tails, source, up_source, down_source, partial, field, total,
           got_near, got_rest, got_far,
           load_sem, send_sem, recv_sem):
    me = lax.axis_index("row")
    r = p.radius
    has_up, has_down = me > 0, me < devices - 1
    has_up2, has_down2 = me > 1, me < devices - 2
    kinds = weight_hbm.shape[1]

    barrier = pltpu.get_barrier_semaphore()

    @pl.when(has_up)
    def _():
        pl.semaphore_signal(barrier, inc=1, device_id={"row": me - 1}, device_id_type=MESH)

    @pl.when(has_down)
    def _():
        pl.semaphore_signal(barrier, inc=1, device_id={"row": me + 1}, device_id_type=MESH)

    pairs = ((mask_hbm, field.at[pl.ds(r, p.rows)]), (target_hbm, target_ref.at[pl.ds(r, p.rows)]),
             (taps_hbm, taps), (hot_hbm, hot_ref), (count_hbm, count_ref), (weight_hbm, weight_ref))
    loads = [pltpu.make_async_copy(a, b, load_sem.at[k]) for k, (a, b) in enumerate(pairs)]
    for load in loads:
        load.start()

    def copies(stage, reach, up_src, down_src, above, below):
        up = pltpu.make_async_remote_copy(
            src_ref=up_src, dst_ref=below, send_sem=send_sem.at[stage, 0],
            recv_sem=recv_sem.at[stage, 0], device_id={"row": me - reach}, device_id_type=MESH)
        down = pltpu.make_async_remote_copy(
            src_ref=down_src, dst_ref=above, send_sem=send_sem.at[stage, 1],
            recv_sem=recv_sem.at[stage, 1], device_id={"row": me + reach}, device_id_type=MESH)
        return reach, up, down

    def start(pair):
        reach, up, down = pair

        @pl.when(me >= reach)
        def _():
            up.start()

        @pl.when(me < devices - reach)
        def _():
            down.start()

    def finish(pair):
        reach, up, down = pair

        @pl.when(me >= reach)
        def _():
            up.wait_send()
            down.wait_recv()

        @pl.when(me < devices - reach)
        def _():
            down.wait_send()
            up.wait_recv()

    def clear(ref, where):
        ref[where] = jnp.zeros(ref.at[where].shape, ref.dtype)

    spot = lax.broadcasted_iota(jnp.int32, (1, p.depth), 1)
    in_tail = spot >= 3 * LANES
    inside = spot & (LANES - 1)
    tap_row = jnp.where(in_tail, inside, (spot // LANES) * r + (inside & (r - 1)))
    tap_col = jnp.where(in_tail, p.side - 1, inside // r)
    wanted = jnp.where(tap_row < p.side, tap_row * p.lane_step + tap_col, -1)
    place = (lax.broadcasted_iota(jnp.int32, (p.packed, p.depth), 0) == wanted).astype(F32).astype(BF16)

    inner = has_up & has_down

    loads[0].wait()

    @pl.when(inner)
    def _():
        pl.semaphore_wait(barrier, 2)

    @pl.when(jnp.logical_not(inner))
    def _():
        pl.semaphore_wait(barrier, 1)

    first = copies(0, 1, field.at[pl.ds(r, r)], field.at[pl.ds(p.rows, r)],
                   field.at[pl.ds(0, r)], field.at[pl.ds(r + p.rows, r)])
    start(first)
    aims = copies(1, 1, target_hbm.at[pl.ds(0, r)], target_hbm.at[pl.ds(p.rows - r, r)],
                  target_ref.at[pl.ds(0, r)], target_ref.at[pl.ds(r + p.rows, r)])
    start(aims)

    @pl.when(jnp.logical_not(has_up))
    def _():
        clear(field, pl.ds(0, r))
        clear(target_ref, pl.ds(0, r))
        clear(got_near, 0)
        clear(got_rest, 0)

    @pl.when(jnp.logical_not(has_down))
    def _():
        clear(field, pl.ds(r + p.rows, r))
        clear(target_ref, pl.ds(r + p.rows, r))
        clear(got_near, 1)
        clear(got_rest, 1)

    @pl.when(jnp.logical_not(has_up2))
    def _():
        clear(got_far, 0)

    @pl.when(jnp.logical_not(has_down2))
    def _():
        clear(got_far, 1)

    pack[...] = jnp.zeros(pack.shape, F32)
    for load in loads[1:]:
        load.wait()

    for c in range(p.corners):
        for a in range(p.side):
            pack[pl.ds(c * p.channels, p.channels), pl.ds(a * p.lane_step, p.side)] = (
                taps[c, a].astype(F32))
    base = jnp.dot(pack[...].astype(BF16), place, preferred_element_type=F32)
    lane = lax.broadcasted_iota(jnp.int32, (1, r, LANES), 2)
    phase = lax.broadcasted_iota(jnp.int32, (1, r, LANES), 1)
    straight = (lane & (r - 1)) + phase < r
    for c in range(p.corners):
        span = slice(c * p.channels, (c + 1) * p.channels)
        base_ref[c, :, pl.ds(0, p.depth)] = base[span]
        for q in range(2):
            base_ref[c, :, pl.ds((4 + q) * LANES, LANES)] = pltpu.roll(
                base[span, q * LANES : (q + 1) * LANES], LANES - r, 1)

    def spread_out(chosen, into):
        def wide(c, q):
            part = base_ref[c, :, pl.ds(q * LANES, LANES)]
            return jnp.broadcast_to(part[:, None, :], (p.channels, r, LANES))

        for s in range(p.slots):
            for q in range(4):
                here = wide(chosen[s], q)
                if q < 3:
                    here = jnp.where(straight, here, wide(chosen[s], q + 3) if q else 0.0)
                turned = pltpu.roll(here, 0, 2, stride=1, stride_axis=1)
                into[pl.ds(s * p.slot_rows, p.slot_rows), pl.ds(q * LANES, LANES)] = (
                    turned.reshape(p.slot_rows, LANES).astype(BF16))
        if p.mix > p.used:
            clear(into, pl.ds(p.used, p.mix - p.used))

    up_tile, down_tile = jnp.maximum(me - 1, 0), jnp.minimum(me + 1, devices - 1)
    corners = [hot_ref[s, me] for s in range(p.slots)]
    up_corners = [hot_ref[s, up_tile] for s in range(p.slots)]
    down_corners = [hot_ref[s, down_tile] for s in range(p.slots)]
    count = count_ref[me]
    up_count = jnp.where(has_up, count_ref[up_tile], 0)
    down_count = jnp.where(has_down, count_ref[down_tile], 0)

    def turn(whole, quarters, into):
        for q in range(p.mix // 256):
            for n, quarter in enumerate(quarters):
                tall = p.tail if quarter == 3 else LANES
                turned = whole[pl.ds(q * 256, 256), pl.ds(quarter * LANES, LANES)].astype(F32).T
                into[pl.ds(n * LANES, tall), pl.ds(q * 256, 256)] = turned[:tall].astype(BF16)

    for ref in (source, up_source, down_source):
        if p.mix > p.used:
            clear(ref, pl.ds(p.used, p.mix - p.used))
    spread_out(corners, own_big)
    turn(own_big, (0, 1, 2, 3), own_t)

    def lay(value, which):
        for b in range(0, p.side - 1, 2):
            left, right = shifted(value, r - b), shifted(value, r - b - 1)
            for n, i in enumerate(which):
                rows = slice(n * r, (n + 1) * r)
                blocks[pl.ds(i * LANES + b * r, 2 * r), :] = (
                    jnp.concatenate([left[rows], right[rows]], axis=0).astype(BF16))

    def lay_tails(value, which):
        last = shifted(value, r - p.side + 1)
        for n, g in enumerate(which):
            padded = jnp.concatenate([last[n * r : (n + 3) * r], jnp.zeros((r, p.width), F32)], axis=0)
            tails[g] = padded.astype(BF16)

    def patch(g):
        return jnp.concatenate([blocks[pl.ds(g * LANES, 3 * LANES), :], tails[g]], axis=0)

    def excite(s, image, n, chosen, limit, aim, into):
        image = image.reshape(p.channels, r, n)
        weights = [weight_ref[chosen[s], k] for k in range(kinds)]
        intensity = jnp.zeros((r, n), F32)
        for k in range(kinds):
            both_parts = image[k] * image[k] + image[k + kinds] * image[k + kinds]
            intensity = intensity + weights[k] * both_parts
        resist = jax.nn.sigmoid(STEEPNESS * (intensity - THRESHOLD))
        slope = 2.0 * (resist - aim) * STEEPNESS * resist * (1.0 - resist)
        slope = jnp.where(s < limit, slope, 0.0)
        scaled = [(2.0 * weights[k]) * slope for k in range(kinds)]
        sent = jnp.stack([scaled[j % kinds] * image[j] for j in range(p.channels)])
        into[pl.ds(s * p.slot_rows, p.slot_rows), :] = sent.reshape(p.slot_rows, n).astype(BF16)

    def forward(groups, whole, chosen, limit, aim, into):
        patches = jnp.concatenate([patch(g) for g in groups], axis=1)
        for s in range(p.slots):
            image = jnp.dot(whole[pl.ds(s * p.slot_rows, p.slot_rows), pl.ds(0, p.deep)], patches,
                            preferred_element_type=F32)
            excite(s, image, len(groups) * p.width, chosen, limit, aim, into)

    def forward_own_rows():
        inner_blocks = blocks[pl.ds(2 * LANES, 2 * LANES), :]
        for g in range(2):
            partial[:, pl.ds(g * p.width, p.width)] = jnp.dot(
                own_big[pl.ds(0, p.used), pl.ds((1 - g) * LANES, 2 * LANES)], inner_blocks,
                preferred_element_type=F32)

    def forward_halo_rows(aim):
        for s in range(p.slots):
            rows = pl.ds(s * p.slot_rows, p.slot_rows)
            both = []
            for g in range(2):
                left = jnp.concatenate([own_big[rows, pl.ds(2 * g * LANES, LANES)],
                                        own_big[rows, pl.ds(3 * LANES, p.tail)]], axis=1)
                right = jnp.concatenate([blocks[pl.ds((1 + 3 * g) * LANES, LANES), :], tails[1 + g]], axis=0)
                both.append(jnp.dot(left, right, preferred_element_type=F32))
            image = partial[rows, :] + jnp.concatenate(both, axis=1)
            excite(s, image, 2 * p.width, corners, count, aim, source)

    def gathered(rows_of):
        sums = 0.0
        for b in range(p.side):
            sums = sums + shifted(jnp.concatenate(rows_of(b), axis=0), b - r)
        return sums

    def third(value, w, b, base=0):
        at = (w - base) * LANES + b * r if b < p.side - 1 else (3 - base) * LANES + w * r
        return value[at : at + r]

    lay(field[pl.ds(r, p.rows), :].astype(BF16).astype(F32), (2, 3))
    finish(first)
    aim = jnp.concatenate([target_ref[pl.ds((g + 1) * r, r), :] for g in range(2)], axis=1)
    low = field[...].astype(BF16).astype(F32)
    lay(jnp.concatenate([low[:r], low[r + p.rows :]], axis=0), (1, 4))
    lay_tails(low, (1, 2))
    forward((1, 2), own_big, corners, count, aim, source)
    spread = [jnp.dot(own_t[...], source[:, pl.ds(g * p.width, p.width)], preferred_element_type=F32)
              for g in range(2)]
    lo, hi = spread
    gradient = STEP_RATE * gathered(lambda b: [
        third(lo, 0, b), third(lo, 1, b) + third(hi, 0, b), third(lo, 2, b) + third(hi, 1, b),
        third(hi, 2, b)])
    total[pl.ds(0, r), :] = gradient[:r]
    total[pl.ds(r, p.rows), :] = field[pl.ds(r, p.rows), :] - gradient[r : r + p.rows]
    total[pl.ds(r + p.rows, r), :] = gradient[r + p.rows :]
    near = copies(2, 1, total.at[pl.ds(0, 2 * r)], total.at[pl.ds(2 * r, 2 * r)], got_near.at[0], got_near.at[1])
    start(near)
    rest = copies(3, 1, total.at[pl.ds(2 * r, r)], total.at[pl.ds(r, r)], got_rest.at[0], got_rest.at[1])
    start(rest)
    beyond = copies(4, 2, total.at[pl.ds(0, r)], total.at[pl.ds(3 * r, r)], got_far.at[0], got_far.at[1])
    start(beyond)

    forward((1, 2), own_big, corners, count, aim, source)
    spread_out(up_corners, up_big)
    spread_out(down_corners, down_big)
    turn(up_big, (2, 3), up_t)
    turn(down_big, (0, 3), down_t)
    finish(aims)
    finish(near)
    above, below = got_near[0], got_near[1]
    upper = jnp.where(has_up, total[pl.ds(0, r), :], 0.0)
    lower = jnp.where(has_down, total[pl.ds(3 * r, r), :], 0.0)
    own = total[pl.ds(r, p.rows), :] - jnp.concatenate([above[r:], below[:r]], axis=0)
    after = jnp.concatenate([above[:r] - upper, own, below[r:] - lower], axis=0)
    low = after.astype(BF16).astype(F32)
    lay(low, (1, 2, 3, 4))
    lay_tails(low, (1, 2))
    forward((1, 2), own_big, corners, count, aim, source)
    finish(rest)
    finish(beyond)
    outer = jnp.concatenate([got_rest[0] - got_far[0], got_rest[1] - got_far[1]], axis=0)
    outer = outer.astype(BF16).astype(F32)
    lay(outer, (0, 5))
    lay_tails(jnp.concatenate([outer[:r], low[: 2 * r]], axis=0), (0,))
    lay_tails(jnp.concatenate([low[2 * r :], outer[r:]], axis=0), (3,))
    forward((0,), up_big, up_corners, up_count, target_ref[pl.ds(0, r), :], up_source)
    forward((3,), down_big, down_corners, down_count, target_ref[pl.ds(r + p.rows, r), :], down_source)
    lo = jnp.dot(own_t[pl.ds(LANES, 2 * LANES + p.tail), :], source[:, pl.ds(0, p.width)],
                 preferred_element_type=F32)
    hi = jnp.dot(jnp.concatenate([own_t[pl.ds(0, 2 * LANES), :], own_t[pl.ds(3 * LANES, p.tail), :]], axis=0),
                 source[:, pl.ds(p.width, p.width)], preferred_element_type=F32)
    ups = jnp.dot(up_t[...], up_source[...], preferred_element_type=F32)
    downs = jnp.dot(down_t[...], down_source[...], preferred_element_type=F32)

    def near_rows(b):
        if b < p.side - 1:
            at = b * r
            return [lo[at : at + r] + hi[at : at + r] + ups[at : at + r],
                    lo[LANES + at : LANES + at + r] + hi[LANES + at : LANES + at + r] + downs[at : at + r]]
        x, y = lo[2 * LANES :], hi[2 * LANES :]
        u, d = ups[LANES:], downs[LANES:]
        return [x[r : 2 * r] + y[:r] + u[2 * r : 3 * r], x[2 * r : 3 * r] + y[r : 2 * r] + d[:r]]

    out_ref[...] = own - STEP_RATE * gathered(near_rows)


def body(devices, mask, target, kernels, corner_weights, hotspots, counts):
    rows, width = mask.shape
    p = Plan(rows, width, kernels.shape[0], kernels.shape[1], kernels.shape[-1], hotspots.shape[1])
    assert rows == 2 * p.radius and p.radius == 8 and p.side == 17
    taps = jnp.transpose(kernels, (0, 2, 1, 3))
    vmem = pl.BlockSpec(memory_space=pltpu.VMEM)
    r = p.radius
    return pl.pallas_call(
        functools.partial(kernel, p, devices),
        out_shape=pltpu.VMEM((rows, width), F32),
        in_specs=[pl.BlockSpec(memory_space=pl.ANY)] * 6,
        out_specs=vmem,
        scratch_shapes=[
            pltpu.SMEM(hotspots.shape[::-1], hotspots.dtype),
            pltpu.SMEM(counts.shape, counts.dtype),
            pltpu.SMEM(corner_weights.shape, corner_weights.dtype),
            pltpu.VMEM((p.ext, width), target.dtype),
            pltpu.VMEM(taps.shape, taps.dtype),
            pltpu.VMEM((p.corners * p.channels, p.packed), F32),
            pltpu.VMEM((p.corners, p.channels, 6 * LANES), F32),
            pltpu.VMEM((p.mix, p.depth), BF16),
            pltpu.VMEM((p.mix, p.depth), BF16),
            pltpu.VMEM((p.mix, p.depth), BF16),
            pltpu.VMEM((p.deep, p.mix), BF16),
            pltpu.VMEM((LANES + p.tail, p.mix), BF16),
            pltpu.VMEM((LANES + p.tail, p.mix), BF16),
            pltpu.VMEM((6 * LANES, width), BF16),
            pltpu.VMEM((4, p.tail, width), BF16),
            pltpu.VMEM((p.mix, 2 * width), BF16),
            pltpu.VMEM((p.mix, width), BF16),
            pltpu.VMEM((p.mix, width), BF16),
            pltpu.VMEM((p.used, 2 * width), F32),
            pltpu.VMEM((p.ext, width), F32),
            pltpu.VMEM((p.ext, width), F32),
            pltpu.VMEM((2, 2 * r, width), F32),
            pltpu.VMEM((2, r, width), F32),
            pltpu.VMEM((2, r, width), F32),
            pltpu.SemaphoreType.DMA((6,)),
            pltpu.SemaphoreType.DMA((5, 2)),
            pltpu.SemaphoreType.DMA((5, 2)),
        ],
        compiler_params=pltpu.CompilerParams(collective_id=0, has_side_effects=True),
        name="litho",
    )(hotspots.T, counts, corner_weights, mask, target, taps)


def solution(mesh):
    placed = (
        P(("strip", "row"), None),
        P(("strip", "row"), None),
        P(),
        P(),
        P("strip", None),
        P("strip"),
    )
    return jax.shard_map(
        functools.partial(body, mesh.shape["row"]), mesh=mesh, in_specs=placed,
        out_specs=P(("strip", "row"), None), check_vma=False
    )
```
